32 devices in a mesh: gx: 4 (over y, x), gy: 8 (over z, core).
Axes of the slice: x: 2, y: 2, z: 4, core: 2. Of those that a mesh axis runs over, the one named last changes fastest.
Arguments:
- probes: float32 [24, 48, 64, 128], P('gx', 'gy'), may hold values from -6 to 6
- pair_blocks: float32 [24, 48, 9, 128, 128], P('gx', 'gy'), may hold values from -0.09375 to 0.09375
- partners: int32 [24, 48, 9], P('gx', 'gy'), may hold values from 0 to 1151, as said below
- shifts: int32 [2, 24, 48, 9], P(None, 'gx', 'gy'), may hold values from -1 to 1, as said below
- counts: int32 [24, 48], P('gx', 'gy'), may hold values from 1 to 9, as said below
- kpoint: float32 [2], replicated, may hold values from -3.140625 to 3.140625
Outputs:
- last_vector: float32 [24, 48, 64, 128], P('gx', 'gy')
- intersections: float32 [3, 2, 32], replicated
The draws below stay inside these ranges and needn't reach their ends.
Inputs may be any that keep to these rules, and one draw needn't show every extreme that they name: `partners`: slot 0 of cell (x, y) names the cell itself; slots 1 to 8 name its eight neighbouring cells (x + dx, y + dy) with dx, dy in -1..1 taken periodically modulo 24 and 48, each once, in no fixed order. shifts[0, x, y, s] = (x + dx - px) / 24 and shifts[1, x, y, s] = (y + dy - py) / 48 for the slot's offset (dx, dy) and partner cell (px, py). `counts`: slots at or beyond a cell's count are padding; some cell has all 9 slots live.
All inputs are finite; a program needn't handle non-finite values.
Results may differ from the reference program's by a relative error of at most 0.0001.
Values sent between devices are 32-bit elements; how exact they have to be, the bound alone decides.
A program may use at most 128 MiB of HBM per device.

```python
import math
import jax
import jax.numpy as jnp
from jax import lax

CX = 6
CY = 6
BLOCK = 128
SLOTS = 9
PROBES = 32
STEPS = 3
NCX = 24
NCY = 48
ROWS = 147456


def pair_layout(key):
    base = jax.random.fold_in(key, 7)
    first_key, second_key, third_key = jax.random.split(base, 3)
    bricks_x = NCX // CX
    bricks_y = NCY // CY
    dense_brick = jax.random.randint(first_key, (bricks_x, bricks_y), 0, 2)
    dense_brick = dense_brick.at[0, 0].set(1)
    cell_x = jnp.arange(NCX, dtype=jnp.int32)[:, None]
    cell_y = jnp.arange(NCY, dtype=jnp.int32)[None, :]
    dense = dense_brick[cell_x // CX, cell_y // CY]
    live = jax.random.randint(second_key, (NCX, NCY, 8), 0, 2)
    live = jnp.maximum(live, dense[:, :, None])
    scores = jax.random.randint(third_key, (NCX, NCY, 8), 0, 1 << 20) * 8 + jnp.arange(8, dtype=jnp.int32)
    ranking = (1 - live) * (1 << 24) + scores
    order = jnp.argsort(ranking, axis=-1, stable=True).astype(jnp.int32)
    table_x = jnp.array([-1, -1, -1, 0, 0, 1, 1, 1], jnp.int32)
    table_y = jnp.array([-1, 0, 1, -1, 1, -1, 0, 1], jnp.int32)
    offset_x = jnp.take(table_x, order)
    offset_y = jnp.take(table_y, order)
    zero = jnp.zeros((NCX, NCY, 1), jnp.int32)
    offset_x = jnp.concatenate([zero, offset_x], axis=-1)
    offset_y = jnp.concatenate([zero, offset_y], axis=-1)
    target_x = cell_x[:, :, None] + offset_x
    target_y = cell_y[:, :, None] + offset_y
    partner_x = jnp.mod(target_x, NCX)
    partner_y = jnp.mod(target_y, NCY)
    shift_x = jnp.floor_divide(target_x, NCX)
    shift_y = jnp.floor_divide(target_y, NCY)
    partners = (partner_x * NCY + partner_y).astype(jnp.int32)
    shifts = jnp.stack([shift_x, shift_y]).astype(jnp.int32)
    counts = (1 + jnp.sum(live, axis=-1)).astype(jnp.int32)
    return (partners, shifts, counts)


def draw_partners(key, part):
    return pair_layout(key)[0]


def draw_shifts(key, part):
    return pair_layout(key)[1]


def draw_counts(key, part):
    return pair_layout(key)[2]


def block_levels(stream_key, extent, cuts, least, high):
    factor_of, own = 1.0, jax.random.fold_in(stream_key, 6)
    for position, parts in cuts:
        steps = jnp.exp(jax.random.uniform(jax.random.fold_in(own, position), (parts,), jnp.float32, least / len(cuts), high / len(cuts)))
        factor_of = factor_of * jnp.repeat(steps, extent[position] // parts).reshape([-1 if axis == position else 1 for axis in range(len(extent))])
    return factor_of


def gaussian(own_key, shape, spread, bound, shards=(), kind=jnp.bfloat16):
    gain = block_levels(own_key, shape, shards, -0.22, 0.18) if shards else 1.0
    drawn = jax.random.normal(own_key, shape, jnp.float32) * spread * gain
    return jnp.minimum(jnp.maximum(drawn, -bound), bound).astype(kind)


def setup_inputs(seed: int = 0) -> dict:
    arg_keys = jax.random.split(jax.random.key(seed), 7)
    probes = gaussian(arg_keys[0], (NCX, NCY, 2 * PROBES, BLOCK), 1.0, 6.0, ((0, 4), (1, 8)), jnp.float32)
    pair_blocks = gaussian(arg_keys[1], (NCX, NCY, SLOTS, BLOCK, BLOCK), (4 * BLOCK * SLOTS) ** -0.5, 0.09375, ((0, 4), (1, 8)), jnp.float32)
    partners = draw_partners(jax.random.fold_in(arg_keys[6], 71), 0)
    shifts = draw_shifts(jax.random.fold_in(arg_keys[6], 71), 0)
    counts = draw_counts(jax.random.fold_in(arg_keys[6], 71), 0)
    kpoint = jnp.clip(jax.random.uniform(arg_keys[5], (2,), jnp.float32, -3.140625, 3.140625), -3.140625, 3.140625)
    return dict(probes=probes, pair_blocks=pair_blocks, partners=partners, shifts=shifts, counts=counts, kpoint=kpoint)


def apply_hamiltonian(field, blocks, flat_partner, cosine, sine):
    cells = flat_partner.shape[0]
    width = field.shape[2]
    half = width // 2
    source = field.reshape(cells, width, BLOCK)

    def accumulate(slot, sums):
        real_sum, imag_sum = sums
        piece = jnp.take(source, flat_partner[:, slot], axis=0)
        block = lax.dynamic_index_in_dim(blocks, slot, 1, keepdims=False)
        product = jnp.einsum('npb,nba->npa', piece, block, precision=lax.Precision.HIGHEST)
        cos_part = lax.dynamic_index_in_dim(cosine, slot, 1, keepdims=False)[:, None, None]
        sin_part = lax.dynamic_index_in_dim(sine, slot, 1, keepdims=False)[:, None, None]
        real_part = product[:, :half]
        imag_part = product[:, half:]
        return (real_sum + cos_part * real_part - sin_part * imag_part, imag_sum + sin_part * real_part + cos_part * imag_part)
    zeros = jnp.zeros((cells, half, BLOCK), jnp.float32)
    real_sum, imag_sum = lax.fori_loop(0, SLOTS, accumulate, (zeros, zeros))
    return jnp.concatenate([real_sum, imag_sum], axis=1).reshape(field.shape)

def intersection(first, other):
    half = first.shape[2] // 2
    first_re, first_im = (first[:, :, :half], first[:, :, half:])
    other_re, other_im = (other[:, :, :half], other[:, :, half:])
    real_part = lax.optimization_barrier(jnp.sum(first_re * other_re + first_im * other_im, axis=(0, 1, 3)))
    imag_part = lax.optimization_barrier(jnp.sum(first_re * other_im - first_im * other_re, axis=(0, 1, 3)))
    return jnp.stack([real_part, imag_part])

def reference(probes, pair_blocks, partners, shifts, counts, kpoint):
    cells = NCX * NCY
    flat_partner = partners.reshape(cells, SLOTS).astype(jnp.int32)
    angle = kpoint[0] * shifts[0].astype(jnp.float32) + kpoint[1] * shifts[1].astype(jnp.float32)
    angle = angle.reshape(cells, SLOTS)
    live = (jnp.arange(SLOTS, dtype=jnp.int32)[None, :] < counts.reshape(cells, 1)).astype(jnp.float32)
    cosine = jnp.cos(angle) * live
    sine = jnp.sin(angle) * live
    blocks = pair_blocks.reshape(cells, SLOTS, BLOCK, BLOCK)
    scale = 1.0 / math.sqrt(ROWS)
    before = probes
    current = apply_hamiltonian(probes, blocks, flat_partner, cosine, sine)
    found = [intersection(probes, current) * scale]
    for step in range(STEPS - 1):
        following = 2.0 * apply_hamiltonian(current, blocks, flat_partner, cosine, sine) - before
        before, current = (current, following)
        found.append(intersection(probes, current) * scale)
    return (current, jnp.stack(found))
```

```python
import functools
import math

import jax
import jax.numpy as jnp
from jax import lax
from jax.experimental import pallas as pl
from jax.experimental.pallas import tpu as pltpu
from jax.sharding import PartitionSpec as P

STEPS = 3
MESH = pl.DeviceIdType.MESH
F32, BF16 = jnp.float32, jnp.bfloat16


def kernel(
    axes, table, counts, phase, v0_hbm, blocks_hbm, last, total,
    v0, v1, v2, halo_x, halo_y, field_a, field_b, landed, weights, sums, ring_x, ring_y,
    v0_sem, land_sem, send_sem, recv_sem, sum_send_x, sum_recv_x, sum_send_y, sum_recv_y,
):
    (name_x, size_x), (name_y, size_y) = axes
    cx, cy, width, block = v0.shape
    slots = landed.shape[1]
    half = width // 2
    pitch = cy + 2
    me_x, me_y = lax.axis_index(name_x), lax.axis_index(name_y)
    vectors = (v0, v1, v2, last)
    fields = (field_a, field_b)

    def landing(x, y):
        i = x * cy + y
        return pltpu.make_async_copy(blocks_hbm.at[x, y], landed.at[i], land_sem.at[i])

    def interior(k):
        return 1 + k // (cy - 2), 1 + k % (cy - 2)

    def rim_y(k):
        return 1 + k // 2, (k % 2) * (cy - 1)

    def rim_x(k):
        return (k // (cy - 2)) * (cx - 1), 1 + k % (cy - 2)

    def corner(k):
        return (k // 2) * (cx - 1), (k % 2) * (cy - 1)

    groups = (
        (interior, (cx - 2) * (cy - 2)),
        (rim_y, 2 * (cx - 2)),
        (rim_x, 2 * (cy - 2)),
        (corner, 4),
    )

    load_v0 = pltpu.make_async_copy(v0_hbm, v0, v0_sem)
    load_v0.start()
    for place, count in groups:

        @pl.loop(0, count)
        def _(k):
            landing(*place(k)).start()

    barrier = pltpu.get_barrier_semaphore()
    for name, size, me in ((name_x, size_x, me_x), (name_y, size_y, me_y)):
        for j in range(1, size):
            pl.semaphore_signal(
                barrier, inc=1, device_id={name: lax.rem(me + j, size)}, device_id_type=MESH
            )
    pl.semaphore_wait(barrier, size_x + size_y - 2)

    def towards(name, size, me, side):
        return {name: lax.rem(me + (size - 1 if side else 1), size)}

    def remote(step, kind, src, dst, peer):
        return pltpu.make_async_remote_copy(
            src_ref=src,
            dst_ref=dst,
            send_sem=send_sem.at[step, kind],
            recv_sem=recv_sem.at[step, kind],
            device_id=peer,
            device_id_type=MESH,
        )

    def x_copies(step, part):
        first, length = ((1, cy - 2), (0, 1), (cy - 1, 1))[part]
        return [
            remote(
                step,
                2 * part + side,
                vectors[step].at[0 if side else cx - 1, pl.ds(first, length)],
                halo_x.at[step, side, pl.ds(first, length)],
                towards(name_x, size_x, me_x, side),
            )
            for side in range(2)
        ]

    def y_copies(step):
        return [
            remote(
                step,
                6 + side,
                vectors[step].at[:, 0 if side else cy - 1],
                halo_y.at[step, side, pl.ds(1, cx)],
                towards(name_y, size_y, me_y, side),
            )
            for side in range(2)
        ]

    def corner_copies(step):
        return [
            remote(
                step,
                8 + 2 * side + end,
                halo_x.at[step, end, 0 if side else cy - 1],
                halo_y.at[step, side, end * (cx + 1)],
                towards(name_y, size_y, me_y, side),
            )
            for side in range(2)
            for end in range(2)
        ]

    def start(copies):
        for copy in copies:
            copy.start()

    def arrive(copies):
        for copy in copies:
            copy.wait_recv()

    def put(field, position, value):
        high = value.astype(BF16)
        field[position, :width] = high
        field[position, width:] = (value - high.astype(F32)).astype(BF16)

    def put_turned(field, position, value, at_x, at_y):
        entry = at_x * 3 + at_y
        cosine, sine = phase[entry], phase[9 + entry]
        real, imag = value[:half], value[half:]
        put(
            field,
            position,
            jnp.concatenate(
                [cosine * real - sine * imag, sine * real + cosine * imag], axis=0
            ),
        )

    def prepare(x, y):
        i = x * cy + y
        landing(x, y).wait()
        count = counts[i]
        for s in range(slots):
            entry = landed[i, s] * jnp.where(s < count, 1.0, 0.0).astype(F32)
            high = entry.astype(BF16)
            weights[i, s * block : (s + 1) * block, :block] = high
            weights[i, s * block : (s + 1) * block, block:] = (
                entry - high.astype(F32)
            ).astype(BF16)

    def advance(step, x, y):
        i = x * cy + y
        source = fields[step % 2]
        lhs = jnp.concatenate([source[table[i * slots + s]] for s in range(slots)], axis=1)
        product = jnp.dot(lhs, weights[i], preferred_element_type=F32)
        value = product[:width, :block] + (
            product[width:, :block] + product[:width, block:] + product[width:, block:]
        )
        if step:
            value = 2.0 * value - vectors[step - 1][x, y]
        vectors[step + 1][x, y] = value
        if step + 1 < STEPS:
            put(fields[(step + 1) % 2], (x + 1) * pitch + y + 1, value)
        start_vector = v0[x, y]
        first_re, first_im = start_vector[:half], start_vector[half:]
        other_re, other_im = value[:half], value[half:]
        low = step * width
        sums[low : low + half] += first_re * other_re + first_im * other_im
        sums[low + half : low + width] += first_re * other_im - first_im * other_re

    def run(step, group):
        place, count = groups[group]

        def body(k, carry):
            x, y = place(k)
            if step == 0:
                prepare(x, y)
            advance(step, x, y)
            return carry

        lax.fori_loop(0, count, body, 0, unroll=1 if step == 0 else 2)

    load_v0.wait()
    start(x_copies(0, 1) + x_copies(0, 2) + y_copies(0) + x_copies(0, 0))
    sums[...] = jnp.zeros_like(sums)

    @pl.loop(0, cx * cy)
    def _(k):
        x, y = k // cy, k % cy
        put(field_a, (x + 1) * pitch + y + 1, v0[x, y])

    for step in range(STEPS):
        field = fields[step % 2]
        run(step, 0)
        arrive(y_copies(step))
        for side in range(2):

            @pl.loop(0, cx)
            def _(x):
                put_turned(
                    field,
                    (x + 1) * pitch + side * (cy + 1),
                    halo_y[step, side, x + 1],
                    1,
                    2 * side,
                )

        run(step, 1)
        arrive(x_copies(step, 1) + x_copies(step, 2))
        start(corner_copies(step))
        arrive(x_copies(step, 0))
        for side in range(2):

            @pl.loop(0, cy)
            def _(y):
                put_turned(
                    field,
                    side * (cx + 1) * pitch + y + 1,
                    halo_x[step, side, y],
                    2 * side,
                    1,
                )

        run(step, 2)
        if step + 1 < STEPS:
            start(x_copies(step + 1, 0))
        arrive(corner_copies(step))
        for side in range(2):
            for end in range(2):
                put_turned(
                    field,
                    end * (cx + 1) * pitch + side * (cy + 1),
                    halo_y[step, side, end * (cx + 1)],
                    2 * end,
                    2 * side,
                )
        run(step, 3)
        if step + 1 < STEPS:
            start(x_copies(step + 1, 1) + x_copies(step + 1, 2) + y_copies(step + 1))

    found = lax.dot_general(
        jnp.ones((8, block), F32),
        sums[...],
        (((1,), (1,)), ((), ())),
        precision=lax.Precision.HIGHEST,
        preferred_element_type=F32,
    )
    for name, size, me, ring, sent, got in (
        (name_x, size_x, me_x, ring_x, sum_send_x, sum_recv_x),
        (name_y, size_y, me_y, ring_y, sum_send_y, sum_recv_y),
    ):
        ring[me] = found
        copies = [
            pltpu.make_async_remote_copy(
                src_ref=ring.at[me],
                dst_ref=ring.at[me],
                send_sem=sent.at[j],
                recv_sem=got.at[j],
                device_id={name: lax.rem(me + j, size)},
                device_id_type=MESH,
            )
            for j in range(1, size)
        ]
        start(copies)
        for copy in copies:
            copy.wait()
        found = ring[0]
        for j in range(1, size):
            found = found + ring[j]
    total[...] = found
    for step in range(STEPS):
        for copy in (
            x_copies(step, 0) + x_copies(step, 1) + x_copies(step, 2)
            + y_copies(step) + corner_copies(step)
        ):
            copy.wait_send()


def shards(axes, probes, pair_blocks, partners, shifts, counts, kpoint):
    (name_x, size_x), (name_y, size_y) = axes
    cx, cy, width, block = probes.shape
    slots = pair_blocks.shape[2]
    cells = cx * cy
    total_x, total_y = cx * size_x, cy * size_y
    me_x, me_y = lax.axis_index(name_x), lax.axis_index(name_y)
    at_x = jnp.mod(partners // total_y - me_x * cx + 1, total_x)
    at_y = jnp.mod(partners % total_y - me_y * cy + 1, total_y)
    table = (at_x * (cy + 2) + at_y).reshape(cells * slots)
    side = jnp.arange(3, dtype=jnp.int32)

    def crossing(me, size):
        return jnp.where(
            (side == 0) & (me == 0), -1, jnp.where((side == 2) & (me == size - 1), 1, 0)
        ).astype(F32)

    angle = (
        kpoint[0] * crossing(me_x, size_x)[:, None] + kpoint[1] * crossing(me_y, size_y)[None, :]
    ).reshape(9)
    phase = jnp.concatenate([jnp.cos(angle), jnp.sin(angle)])
    rows = STEPS * width
    halo = (width, block)
    smem = pl.BlockSpec(memory_space=pltpu.SMEM)
    anywhere = pl.BlockSpec(memory_space=pl.ANY)
    vmem = pl.BlockSpec(memory_space=pltpu.VMEM)
    dma = pltpu.SemaphoreType.DMA
    last, found = pl.pallas_call(
        functools.partial(kernel, axes),
        out_shape=(
            jax.ShapeDtypeStruct(probes.shape, F32),
            jax.ShapeDtypeStruct((8, rows), F32),
        ),
        in_specs=[smem, smem, smem, anywhere, anywhere],
        out_specs=(vmem, vmem),
        scratch_shapes=[
            pltpu.VMEM(probes.shape, F32),
            pltpu.VMEM(probes.shape, F32),
            pltpu.VMEM(probes.shape, F32),
            pltpu.VMEM((STEPS, 2, cy) + halo, F32),
            pltpu.VMEM((STEPS, 2, cx + 2) + halo, F32),
            pltpu.VMEM(((cx + 2) * (cy + 2), 2 * width, block), BF16),
            pltpu.VMEM(((cx + 2) * (cy + 2), 2 * width, block), BF16),
            pltpu.VMEM((cells, slots, block, block), F32),
            pltpu.VMEM((cells, slots * block, 2 * block), BF16),
            pltpu.VMEM((rows, block), F32),
            pltpu.VMEM((size_x, 8, rows), F32),
            pltpu.VMEM((size_y, 8, rows), F32),
            dma(()),
            dma((cells,)),
            dma((STEPS, 12)),
            dma((STEPS, 12)),
            dma((size_x,)),
            dma((size_x,)),
            dma((size_y,)),
            dma((size_y,)),
        ],
        compiler_params=pltpu.CompilerParams(
            collective_id=0, has_side_effects=True, vmem_limit_bytes=66_000_000
        ),
    )(table, counts.reshape(cells), phase, probes, pair_blocks)
    scale = 1.0 / math.sqrt(total_x * total_y * block)
    return last, (found[0] * scale).reshape(STEPS, 2, width // 2)


def solution(mesh):
    placed = (
        P("gx", "gy", None, None),
        P("gx", "gy", None, None, None),
        P("gx", "gy", None),
        P(None, "gx", "gy", None),
        P("gx", "gy"),
        P(),
    )
    axes = tuple((name, mesh.shape[name]) for name in ("gx", "gy"))
    return jax.shard_map(
        functools.partial(shards, axes),
        mesh=mesh,
        in_specs=placed,
        out_specs=(P("gx", "gy", None, None), P()),
        check_vma=False,
    )
```

```python
import functools
import math

import jax
import jax.numpy as jnp
from jax import lax
from jax.experimental import pallas as pl
from jax.experimental.pallas import tpu as pltpu
from jax.sharding import PartitionSpec as P

STEPS = 3
MESH = pl.DeviceIdType.MESH
F32, BF16 = jnp.float32, jnp.bfloat16


def kernel(
    axes, partners, counts, kpoint, v0_hbm, blocks_hbm, last, total,
    v0, v1, v2, halo_x, halo_y, field_a, field_b, landed, weights, sums, ring_x, ring_y, table, turns,
    v0_sem, land_sem, send_sem, recv_sem, sum_send_x, sum_recv_x, sum_send_y, sum_recv_y,
):
    (name_x, size_x), (name_y, size_y) = axes
    cx, cy, width, block = v0.shape
    slots = landed.shape[1]
    half = width // 2
    pitch = cy + 2
    me_x, me_y = lax.axis_index(name_x), lax.axis_index(name_y)
    total_x, total_y = cx * size_x, cy * size_y
    vectors = (v0, v1, v2, last)
    fields = (field_a, field_b)

    def landing(x, y):
        i = x * cy + y
        return pltpu.make_async_copy(blocks_hbm.at[x, y], landed.at[i], land_sem.at[i])

    inner = (cx - 2) * (cy - 2)
    early = inner // 2

    def interior(k):
        return 1 + k // (cy - 2), 1 + k % (cy - 2)

    def rim_y(k):
        return 1 + k // 2, (k % 2) * (cy - 1)

    def corner(k):
        return (k // 2) * (cx - 1), (k % 2) * (cy - 1)

    def rim_x_near(k):
        return (k // 2) * (cx - 1), 1 + (k % 2) * (cy - 3)

    def rim_x_middle(k):
        return (k // (cy - 4)) * (cx - 1), 2 + k % (cy - 4)

    groups = (
        (interior, early),
        (rim_y, 2 * (cx - 2)),
        (corner, 4),
        (rim_x_near, 4),
        (rim_x_middle, 2 * (cy - 4)),
        (lambda k: interior(k + early), inner - early),
    )
    ends, near, middle = ((0, 1), (cy - 1, 1)), ((1, 1), (cy - 2, 1)), ((2, cy - 4),)

    load_v0 = pltpu.make_async_copy(v0_hbm, v0, v0_sem)
    load_v0.start()
    for place, count in groups:

        @pl.loop(0, count)
        def _(k):
            landing(*place(k)).start()

    barrier = pltpu.get_barrier_semaphore()
    for name, size, me in ((name_x, size_x, me_x), (name_y, size_y, me_y)):
        for j in range(1, size):
            pl.semaphore_signal(
                barrier, inc=1, device_id={name: lax.rem(me + j, size)}, device_id_type=MESH
            )
    pl.semaphore_wait(barrier, size_x + size_y - 2)

    def towards(name, size, me, side):
        return {name: lax.rem(me + (size - 1 if side else 1), size)}

    def remote(step, kind, src, dst, peer):
        return pltpu.make_async_remote_copy(
            src_ref=src,
            dst_ref=dst,
            send_sem=send_sem.at[step, kind],
            recv_sem=recv_sem.at[step, kind],
            device_id=peer,
            device_id_type=MESH,
        )

    def x_copies(step, parts):
        return [
            remote(
                step,
                2 * (ends + near + middle).index((first, length)) + side,
                vectors[step].at[0 if side else cx - 1, pl.ds(first, length)],
                halo_x.at[step, side, pl.ds(first, length)],
                towards(name_x, size_x, me_x, side),
            )
            for first, length in parts
            for side in range(2)
        ]

    def y_copies(step):
        return [
            remote(
                step,
                10 + side,
                vectors[step].at[:, 0 if side else cy - 1],
                halo_y.at[step, side, pl.ds(1, cx)],
                towards(name_y, size_y, me_y, side),
            )
            for side in range(2)
        ]

    def corner_copies(step):
        return [
            remote(
                step,
                12 + 2 * side + end,
                halo_x.at[step, end, 0 if side else cy - 1],
                halo_y.at[step, side, end * (cx + 1)],
                towards(name_y, size_y, me_y, side),
            )
            for side in range(2)
            for end in range(2)
        ]

    def start(copies):
        for copy in copies:
            copy.start()

    def arrive(copies):
        for copy in copies:
            copy.wait_recv()

    def put(field, position, value):
        high = value.astype(BF16)
        field[position, :width] = high
        field[position, width:] = (value - high.astype(F32)).astype(BF16)

    def put_turned(field, position, value, at_x, at_y):
        entry = at_x * 3 + at_y
        cosine, sine = turns[0, entry : entry + 1], turns[1, entry : entry + 1]
        real, imag = value[:half], value[half:]
        put(
            field,
            position,
            jnp.concatenate(
                [cosine * real - sine * imag, sine * real + cosine * imag], axis=0
            ),
        )

    def prepare(x, y):
        i = x * cy + y
        landing(x, y).wait()
        count = counts[x, y]
        for s in range(slots):
            partner = partners[x, y, s]
            partner_x = (partner * (((1 << 20) + total_y - 1) // total_y)) >> 20
            at_x = partner_x - me_x * cx + 1
            at_x = jnp.where(at_x < 0, at_x + total_x, at_x)
            at_x = jnp.where(at_x >= total_x, at_x - total_x, at_x)
            at_y = partner - partner_x * total_y - me_y * cy + 1
            at_y = jnp.where(at_y < 0, at_y + total_y, at_y)
            at_y = jnp.where(at_y >= total_y, at_y - total_y, at_y)
            table[i * slots + s] = at_x * pitch + at_y
            entry = landed[i, s] * jnp.where(s < count, 1.0, 0.0).astype(F32)
            high = entry.astype(BF16)
            weights[i, s * block : (s + 1) * block, :block] = high
            weights[i, s * block : (s + 1) * block, block:] = (
                entry - high.astype(F32)
            ).astype(BF16)

    def advance(step, x, y):
        i = x * cy + y
        source = fields[step % 2]
        final = (cx + 2) * pitch - 1
        lhs = jnp.concatenate(
            [
                source[jnp.minimum(jnp.maximum(table[i * slots + s], 0), final)]
                for s in range(slots)
            ],
            axis=1,
        )
        product = jnp.dot(lhs, weights[i], preferred_element_type=F32)
        value = product[:width, :block] + (
            product[width:, :block] + product[:width, block:] + product[width:, block:]
        )
        if step:
            value = 2.0 * value - vectors[step - 1][x, y]
        vectors[step + 1][x, y] = value
        if step + 1 < STEPS:
            put(fields[(step + 1) % 2], (x + 1) * pitch + y + 1, value)
        start_vector = v0[x, y]
        first_re, first_im = start_vector[:half], start_vector[half:]
        other_re, other_im = value[:half], value[half:]
        low = step * width
        sums[low : low + half] += first_re * other_re + first_im * other_im
        sums[low + half : low + width] += first_re * other_im - first_im * other_re

    def run(step, group):
        place, count = groups[group]

        def body(k, carry):
            x, y = place(k)
            if step == 0:
                prepare(x, y)
            advance(step, x, y)
            return carry

        lax.fori_loop(0, count, body, 0, unroll=1 if step == 0 else 2)

    load_v0.wait()
    start(x_copies(0, ends) + y_copies(0) + x_copies(0, near) + x_copies(0, middle))
    sums[...] = jnp.zeros_like(sums)
    row = lax.broadcasted_iota(jnp.int32, (16, block), 0)

    def crossing(at, me, size):
        low = (at == 0) & (me == 0)
        high = (at == 2) & (me == size - 1)
        return jnp.where(low, -1.0, jnp.where(high, 1.0, 0.0)).astype(F32)

    angle = kpoint[0] * crossing(row // 3, me_x, size_x)
    angle = angle + kpoint[1] * crossing(row % 3, me_y, size_y)
    turns[0], turns[1] = jnp.cos(angle), jnp.sin(angle)

    @pl.loop(0, cx * cy)
    def _(k):
        x, y = k // cy, k % cy
        put(field_a, (x + 1) * pitch + y + 1, v0[x, y])

    def put_x(step, parts):
        for first, length in parts:
            for y in range(first, first + length):
                for side in range(2):
                    put_turned(
                        fields[step % 2],
                        side * (cx + 1) * pitch + y + 1,
                        halo_x[step, side, y],
                        2 * side,
                        1,
                    )

    for step in range(STEPS):
        field = fields[step % 2]
        more = step + 1 < STEPS
        run(step, 0)
        if not more:
            run(step, 5)
        arrive(x_copies(step, ends))
        start(corner_copies(step))
        put_x(step, ends)
        arrive(y_copies(step))
        for side in range(2):

            @pl.loop(0, cx)
            def _(x):
                put_turned(
                    field,
                    (x + 1) * pitch + side * (cy + 1),
                    halo_y[step, side, x + 1],
                    1,
                    2 * side,
                )

        run(step, 1)
        arrive(x_copies(step, near))
        put_x(step, near)
        arrive(corner_copies(step))
        for side in range(2):
            for end in range(2):
                put_turned(
                    field,
                    end * (cx + 1) * pitch + side * (cy + 1),
                    halo_y[step, side, end * (cx + 1)],
                    2 * end,
                    2 * side,
                )
        run(step, 2)
        if more:
            start(x_copies(step + 1, ends) + y_copies(step + 1))
        arrive(x_copies(step, middle))
        put_x(step, middle)
        run(step, 3)
        if more:
            start(x_copies(step + 1, near))
        run(step, 4)
        if more:
            start(x_copies(step + 1, middle))
            run(step, 5)

    found = lax.dot_general(
        jnp.ones((8, block), F32),
        sums[...],
        (((1,), (1,)), ((), ())),
        precision=lax.Precision.HIGHEST,
        preferred_element_type=F32,
    )
    for name, size, me, ring, sent, got in (
        (name_x, size_x, me_x, ring_x, sum_send_x, sum_recv_x),
        (name_y, size_y, me_y, ring_y, sum_send_y, sum_recv_y),
    ):
        ring[me] = found
        copies = [
            pltpu.make_async_remote_copy(
                src_ref=ring.at[me],
                dst_ref=ring.at[me],
                send_sem=sent.at[j],
                recv_sem=got.at[j],
                device_id={name: lax.rem(me + j, size)},
                device_id_type=MESH,
            )
            for j in range(1, size)
        ]
        start(copies)
        for copy in copies:
            copy.wait()
        found = ring[0]
        for j in range(1, size):
            found = found + ring[j]
    total[...] = found
    for step in range(STEPS):
        for copy in (
            x_copies(step, ends + near + middle) + y_copies(step) + corner_copies(step)
        ):
            copy.wait_send()


def shards(axes, probes, pair_blocks, partners, shifts, counts, kpoint):
    (name_x, size_x), (name_y, size_y) = axes
    cx, cy, width, block = probes.shape
    slots = pair_blocks.shape[2]
    cells = cx * cy
    total_x, total_y = cx * size_x, cy * size_y
    rows = STEPS * width
    halo = (width, block)
    smem = pl.BlockSpec(memory_space=pltpu.SMEM)
    anywhere = pl.BlockSpec(memory_space=pl.ANY)
    vmem = pl.BlockSpec(memory_space=pltpu.VMEM)
    dma = pltpu.SemaphoreType.DMA
    last, found = pl.pallas_call(
        functools.partial(kernel, axes),
        out_shape=(
            jax.ShapeDtypeStruct(probes.shape, F32),
            jax.ShapeDtypeStruct((8, rows), F32),
        ),
        in_specs=[smem, smem, smem, anywhere, anywhere],
        out_specs=(vmem, vmem),
        scratch_shapes=[
            pltpu.VMEM(probes.shape, F32),
            pltpu.VMEM(probes.shape, F32),
            pltpu.VMEM(probes.shape, F32),
            pltpu.VMEM((STEPS, 2, cy) + halo, F32),
            pltpu.VMEM((STEPS, 2, cx + 2) + halo, F32),
            pltpu.VMEM(((cx + 2) * (cy + 2), 2 * width, block), BF16),
            pltpu.VMEM(((cx + 2) * (cy + 2), 2 * width, block), BF16),
            pltpu.VMEM((cells, slots, block, block), F32),
            pltpu.VMEM((cells, slots * block, 2 * block), BF16),
            pltpu.VMEM((rows, block), F32),
            pltpu.VMEM((size_x, 8, rows), F32),
            pltpu.VMEM((size_y, 8, rows), F32),
            pltpu.SMEM((cells * slots,), jnp.int32),
            pltpu.VMEM((2, 16, block), F32),
            dma(()),
            dma((cells,)),
            dma((STEPS, 16)),
            dma((STEPS, 16)),
            dma((size_x,)),
            dma((size_x,)),
            dma((size_y,)),
            dma((size_y,)),
        ],
        compiler_params=pltpu.CompilerParams(
            collective_id=0, has_side_effects=True, vmem_limit_bytes=66_000_000
        ),
    )(partners, counts, kpoint, probes, pair_blocks)
    scale = 1.0 / math.sqrt(total_x * total_y * block)
    return last, (found[0] * scale).reshape(STEPS, 2, width // 2)


def solution(mesh):
    placed = (
        P("gx", "gy", None, None),
        P("gx", "gy", None, None, None),
        P("gx", "gy", None),
        P(None, "gx", "gy", None),
        P("gx", "gy"),
        P(),
    )
    axes = tuple((name, mesh.shape[name]) for name in ("gx", "gy"))
    return jax.shard_map(
        functools.partial(shards, axes),
        mesh=mesh,
        in_specs=placed,
        out_specs=(P("gx", "gy", None, None), P()),
        check_vma=False,
    )
```
